32 devices in a mesh: seq: 2 (over core), dp: 4 (over z), group: 4 (over y, x).
Axes of the slice: x: 2, y: 2, z: 4, core: 2. Of those that a mesh axis runs over, the one named last changes fastest.
Arguments:
- hidden_in: float32 [16, 1024, 768], P(('dp', 'group'), 'seq'), may hold values from -6 to 6
- out_grad: float32 [16, 1024, 768], P(('dp', 'group'), 'seq'), may hold values from -6 to 6
- prenorm: float32 [768], P(('seq', 'dp', 'group')), may hold values from 0.5 to 1.5
- inproj: float32 [768, 3352], P(('seq', 'dp', 'group')), may hold values from -0.21875 to 0.21875
- kernels: float32 [4, 1792], P(None, ('seq', 'dp', 'group')), may hold values from -3 to 3
- convbias: float32 [1792], P(('seq', 'dp', 'group')), may hold values from -3 to 3
- stepbias: float32 [24], replicated, may hold values from -9 to -4
- decaylog: float32 [24], replicated, may hold values from 0 to 1.5
- skipgain: float32 [24], replicated, may hold values from 0.5 to 1.5
- gatenorm: float32 [1536], P(('seq', 'dp', 'group')), may hold values from 0.5 to 1.5
- outproj: float32 [1536, 768], P(('seq', 'dp', 'group')), may hold values from -0.15625 to 0.15625
- first_prenorm: float32 [768], P(('seq', 'dp', 'group')), may hold values from -192 to 192
- second_prenorm: float32 [768], P(('seq', 'dp', 'group')), may hold values from 20 to 500
- first_inproj: float32 [768, 3352], P(('seq', 'dp', 'group')), may hold values from -192 to 192
- second_inproj: float32 [768, 3352], P(('seq', 'dp', 'group')), may hold values from 20 to 500
- first_kernels: float32 [4, 1792], P(None, ('seq', 'dp', 'group')), may hold values from -192 to 192
- second_kernels: float32 [4, 1792], P(None, ('seq', 'dp', 'group')), may hold values from 20 to 500
- first_convbias: float32 [1792], P(('seq', 'dp', 'group')), may hold values from -192 to 192
- second_convbias: float32 [1792], P(('seq', 'dp', 'group')), may hold values from 20 to 500
- first_stepbias: float32 [24], replicated, may hold values from -192 to 192
- second_stepbias: float32 [24], replicated, may hold values from 20 to 500
- first_decaylog: float32 [24], replicated, may hold values from -192 to 192
- second_decaylog: float32 [24], replicated, may hold values from 20 to 500
- first_skipgain: float32 [24], replicated, may hold values from -192 to 192
- second_skipgain: float32 [24], replicated, may hold values from 20 to 500
- first_gatenorm: float32 [1536], P(('seq', 'dp', 'group')), may hold values from -192 to 192
- second_gatenorm: float32 [1536], P(('seq', 'dp', 'group')), may hold values from 20 to 500
- first_outproj: float32 [1536, 768], P(('seq', 'dp', 'group')), may hold values from -192 to 192
- second_outproj: float32 [1536, 768], P(('seq', 'dp', 'group')), may hold values from 20 to 500
Outputs:
- block_out: float32 [16, 1024, 768], P(('dp', 'group'), 'seq')
- hidden_grad: float32 [16, 1024, 768], P(('dp', 'group'), 'seq')
- grad_prenorm: float32 [768], P(('seq', 'dp', 'group'))
- grad_inproj: float32 [768, 3352], P(('seq', 'dp', 'group'))
- grad_kernels: float32 [4, 1792], P(None, ('seq', 'dp', 'group'))
- grad_convbias: float32 [1792], P(('seq', 'dp', 'group'))
- grad_stepbias: float32 [24], replicated
- grad_decaylog: float32 [24], replicated
- grad_skipgain: float32 [24], replicated
- grad_gatenorm: float32 [1536], P(('seq', 'dp', 'group'))
- grad_outproj: float32 [1536, 768], P(('seq', 'dp', 'group'))
- change_prenorm: float32 [768], P(('seq', 'dp', 'group'))
- new_inproj: float32 [768, 3352], P(('seq', 'dp', 'group'))
- change_kernels: float32 [4, 1792], P(None, ('seq', 'dp', 'group'))
- change_convbias: float32 [1792], P(('seq', 'dp', 'group'))
- change_stepbias: float32 [24], replicated
- change_decaylog: float32 [24], replicated
- change_skipgain: float32 [24], replicated
- change_gatenorm: float32 [1536], P(('seq', 'dp', 'group'))
- new_outproj: float32 [1536, 768], P(('seq', 'dp', 'group'))
- newfirst_prenorm: float32 [768], P(('seq', 'dp', 'group'))
- newsecond_prenorm: float32 [768], P(('seq', 'dp', 'group'))
- newfirst_inproj: float32 [768, 3352], P(('seq', 'dp', 'group'))
- newsecond_inproj: float32 [768, 3352], P(('seq', 'dp', 'group'))
- newfirst_kernels: float32 [4, 1792], P(None, ('seq', 'dp', 'group'))
- newsecond_kernels: float32 [4, 1792], P(None, ('seq', 'dp', 'group'))
- newfirst_convbias: float32 [1792], P(('seq', 'dp', 'group'))
- newsecond_convbias: float32 [1792], P(('seq', 'dp', 'group'))
- newfirst_stepbias: float32 [24], replicated
- newsecond_stepbias: float32 [24], replicated
- newfirst_decaylog: float32 [24], replicated
- newsecond_decaylog: float32 [24], replicated
- newfirst_skipgain: float32 [24], replicated
- newsecond_skipgain: float32 [24], replicated
- newfirst_gatenorm: float32 [1536], P(('seq', 'dp', 'group'))
- newsecond_gatenorm: float32 [1536], P(('seq', 'dp', 'group'))
- newfirst_outproj: float32 [1536, 768], P(('seq', 'dp', 'group'))
- newsecond_outproj: float32 [1536, 768], P(('seq', 'dp', 'group'))
The draws below stay inside these ranges and needn't reach their ends.
All inputs are finite; a program needn't handle non-finite values.
Results may differ from the reference program's by a relative error of at most 0.012.
The reference program's roundings to bfloat16 on the way count: a program that leaves them out, or rounds other values in their place, can miss the bound.
Values may be sent and summed in bfloat16 or wider, within the bound.
No kernel may reach another device: no remote copies, remote signals or barrier semaphores. Data moves between devices by JAX's collectives and lax.ppermute only.
A program may use at most 192 MiB of HBM per device.

```python
import math
import jax
import jax.numpy as jnp
from jax import lax

D = 768
H = 24
P_SIZE = 64
N = 128
K = 4
BLOCK = 256
STEP = 4
DI = 1536
CONV = 1792
PROJ = 3352
SEQS = 16
LEN = 1024


def levels(own_key, dims, shards, smallest, top_value):
    gain = 1.0
    for position, shards_of in shards:
        heights = jax.random.uniform(jax.random.fold_in(jax.random.fold_in(own_key, 6), position), (shards_of,), jnp.float32, smallest / len(shards), top_value / len(shards))
        gain = gain * jnp.repeat(jnp.exp(heights), dims[position] // shards_of).reshape((-1,) + (1,) * (len(dims) - 1 - position))
    return gain


def centred(key, dims, scale, limit, split=(), kind=jnp.bfloat16):
    drawn = scale * jax.random.normal(key, dims, jnp.float32)
    if split:
        drawn = drawn * levels(key, dims, split, -0.22, 0.18)
    return jnp.clip(drawn, -limit, limit).astype(kind)


def setup_inputs(seed: int = 0) -> dict:
    keys = jax.random.split(jax.random.key(seed), 30)
    hidden_in = centred(keys[0], (SEQS, LEN, D), 1.0, 6.0, ((0, 16), (1, 2)), jnp.float32)
    out_grad = centred(keys[1], (SEQS, LEN, D), 1.0, 6.0, ((0, 16), (1, 2)), jnp.float32)
    prenorm = jnp.clip(1.0 + 0.1 * jax.random.normal(keys[2], (D,), jnp.float32), 0.5, 1.5)
    inproj = centred(keys[3], (D, PROJ), D ** -0.5, 0.21875, ((0, 32),), jnp.float32)
    kernels = centred(keys[4], (K, CONV), K ** -0.5, 3.0, ((1, 32),), jnp.float32)
    convbias = centred(keys[5], (CONV,), 0.5, 3.0, ((0, 32),), jnp.float32)
    stepbias = jnp.clip(jax.random.uniform(keys[6], (H,), jnp.float32, -9.0, -4.0), -9.0, -4.0)
    decaylog = jnp.clip(jax.random.uniform(keys[7], (H,), jnp.float32, 0.0, 1.5), 0.0, 1.5)
    skipgain = jnp.clip(jax.random.uniform(keys[8], (H,), jnp.float32, 0.5, 1.5), 0.5, 1.5)
    gatenorm = jnp.clip(1.0 + 0.1 * jax.random.normal(keys[9], (DI,), jnp.float32), 0.5, 1.5)
    outproj = centred(keys[10], (DI, D), DI ** -0.5, 0.15625, ((0, 32),), jnp.float32)
    first_prenorm = centred(keys[11], (D,), 30.0, 192.0, ((0, 32),), jnp.float32)
    second_prenorm = jnp.clip(jnp.exp(math.log(500.0) - 3.218876 * jax.random.uniform(keys[12], (D,), jnp.float32) ** levels(keys[12], (D,), ((0, 32),), -0.2, 0.2)), 20.0, 500.0)
    first_inproj = centred(keys[13], (D, PROJ), 30.0, 192.0, ((0, 32),), jnp.float32)
    second_inproj = jnp.clip(jnp.exp(math.log(500.0) - 3.218876 * jax.random.uniform(keys[14], (D, PROJ), jnp.float32) ** levels(keys[14], (D, PROJ), ((0, 32),), -0.2, 0.2)), 20.0, 500.0)
    first_kernels = centred(keys[15], (K, CONV), 30.0, 192.0, ((1, 32),), jnp.float32)
    second_kernels = jnp.clip(jnp.exp(math.log(500.0) - 3.218876 * jax.random.uniform(keys[16], (K, CONV), jnp.float32) ** levels(keys[16], (K, CONV), ((1, 32),), -0.2, 0.2)), 20.0, 500.0)
    first_convbias = centred(keys[17], (CONV,), 30.0, 192.0, ((0, 32),), jnp.float32)
    second_convbias = jnp.clip(jnp.exp(math.log(500.0) - 3.218876 * jax.random.uniform(keys[18], (CONV,), jnp.float32) ** levels(keys[18], (CONV,), ((0, 32),), -0.2, 0.2)), 20.0, 500.0)
    first_stepbias = centred(keys[19], (H,), 30.0, 192.0, (), jnp.float32)
    second_stepbias = jnp.clip(jnp.exp(jax.random.uniform(keys[20], (H,), jnp.float32, math.log(20.0), math.log(500.0))), 20.0, 500.0)
    first_decaylog = centred(keys[21], (H,), 30.0, 192.0, (), jnp.float32)
    second_decaylog = jnp.clip(jnp.exp(jax.random.uniform(keys[22], (H,), jnp.float32, math.log(20.0), math.log(500.0))), 20.0, 500.0)
    first_skipgain = centred(keys[23], (H,), 30.0, 192.0, (), jnp.float32)
    second_skipgain = jnp.clip(jnp.exp(jax.random.uniform(keys[24], (H,), jnp.float32, math.log(20.0), math.log(500.0))), 20.0, 500.0)
    first_gatenorm = centred(keys[25], (DI,), 30.0, 192.0, ((0, 32),), jnp.float32)
    second_gatenorm = jnp.clip(jnp.exp(math.log(500.0) - 3.218876 * jax.random.uniform(keys[26], (DI,), jnp.float32) ** levels(keys[26], (DI,), ((0, 32),), -0.2, 0.2)), 20.0, 500.0)
    first_outproj = centred(keys[27], (DI, D), 30.0, 192.0, ((0, 32),), jnp.float32)
    second_outproj = jnp.clip(jnp.exp(math.log(500.0) - 3.218876 * jax.random.uniform(keys[28], (DI, D), jnp.float32) ** levels(keys[28], (DI, D), ((0, 32),), -0.2, 0.2)), 20.0, 500.0)
    return {"hidden_in": hidden_in, "out_grad": out_grad, "prenorm": prenorm, "inproj": inproj, "kernels": kernels, "convbias": convbias, "stepbias": stepbias, "decaylog": decaylog, "skipgain": skipgain, "gatenorm": gatenorm, "outproj": outproj, "first_prenorm": first_prenorm, "second_prenorm": second_prenorm, "first_inproj": first_inproj, "second_inproj": second_inproj, "first_kernels": first_kernels, "second_kernels": second_kernels, "first_convbias": first_convbias, "second_convbias": second_convbias, "first_stepbias": first_stepbias, "second_stepbias": second_stepbias, "first_decaylog": first_decaylog, "second_decaylog": second_decaylog, "first_skipgain": first_skipgain, "second_skipgain": second_skipgain, "first_gatenorm": first_gatenorm, "second_gatenorm": second_gatenorm, "first_outproj": first_outproj, "second_outproj": second_outproj}


eps_norm = 1e-05
beta_first = 0.9
beta_second = 0.999
adam_eps = 1e-08
learn_rate = 0.01
decay_matrix = 0.1
highest = lax.Precision.HIGHEST

def depthwise(padded, kernels_f, convbias_f):
    length = padded.shape[0] - kernels_f.shape[0] + 1
    result = jnp.zeros((length, padded.shape[1]), jnp.float32) + convbias_f[None, :]
    for offset in range(kernels_f.shape[0]):
        result = result + kernels_f[offset][None, :] * padded[offset:offset + length]
    return result

def run_blocks(values, b_proj, c_proj, step_size, logdec, incoming):
    length = values.shape[0]
    nblocks = length // BLOCK
    nheads = step_size.shape[0]
    headdim = incoming.shape[1]
    v_all = values.reshape(nblocks, BLOCK, nheads, headdim)
    b_all = b_proj.reshape(nblocks, BLOCK, b_proj.shape[1])
    c_all = c_proj.reshape(nblocks, BLOCK, c_proj.shape[1])
    s_all = step_size.reshape(nheads, nblocks, BLOCK).transpose(1, 0, 2)
    l_all = logdec.reshape(nheads, nblocks, BLOCK).transpose(1, 0, 2)
    positions = jnp.arange(BLOCK)
    lower_mask = positions[:, None] >= positions[None, :]
    upper_ones = (positions[:, None] <= positions[None, :]).astype(jnp.float32)

    def advance(carried, inputs):
        states, offsets = carried
        v_blk, b_blk, c_blk, s_blk, l_blk = inputs
        cumlog = jnp.dot(l_blk, upper_ones, precision=highest)
        log_diffs = cumlog[:, :, None] - cumlog[:, None, :]
        kept_diff = jnp.where(lower_mask[None], log_diffs, 0.0)
        decays = jnp.where(lower_mask[None], jnp.exp(kept_diff), 0.0)
        gram_mat = jnp.dot(c_blk, b_blk.T, precision=highest)
        mixing = decays * gram_mat[None] * s_blk[:, None, :]
        inner_out = jnp.einsum('hts,shp->thp', mixing, v_blk, precision=highest)
        from_states = jnp.einsum('tn,hpn->thp', c_blk, states, precision=highest) * jnp.exp(cumlog).T[:, :, None]
        tail_decay = jnp.exp(cumlog[:, -1:] - cumlog) * s_blk
        fresh_state = jnp.einsum('shp,sn->hpn', v_blk * tail_decay.T[:, :, None], b_blk, precision=highest)
        states_new = jnp.exp(cumlog[:, -1])[:, None, None] * states + fresh_state
        return ((states_new, offsets + cumlog[:, -1]), (inner_out + from_states, cumlog + offsets[:, None]))
    start_carry = (incoming, jnp.zeros((nheads,), jnp.float32))
    (final_state, ignored), (outputs, cumlogs) = lax.scan(jax.checkpoint(advance), start_carry, (v_all, b_all, c_all, s_all, l_all))
    outputs = outputs.reshape(length, nheads, headdim)
    cumdev = cumlogs.transpose(1, 0, 2).reshape(nheads, length)
    return (outputs, final_state, cumdev)

def front(mixer_in, prior_rows, kernels_f, convbias_f, stepbias, decaylog):
    conv_width = kernels_f.shape[1]
    conv_in = mixer_in[:, :conv_width]
    step_raw = mixer_in[:, conv_width:]
    padded = jnp.concatenate([prior_rows, conv_in], axis=0)
    conv_out = jax.nn.silu(depthwise(padded, kernels_f, convbias_f))
    values = conv_out[:, :DI]
    b_proj = conv_out[:, DI:DI + N]
    c_proj = conv_out[:, DI + N:]
    step_size = jax.nn.softplus(step_raw + stepbias[None, :]).T
    logdec = -step_size * jnp.exp(decaylog)[:, None]
    incoming = jnp.zeros((H, P_SIZE, N), jnp.float32)
    outputs, final_state, cumdev = run_blocks(values, b_proj, c_proj, step_size, logdec, incoming)
    decay_total = jnp.exp(lax.optimization_barrier(jnp.sum(logdec, axis=1)))
    return (outputs, values, c_proj, cumdev, final_state, decay_total)

def gated_norm(flat_rows, gate_part, gatenorm_f):
    gated = flat_rows * jax.nn.silu(gate_part)
    return gated * lax.rsqrt(lax.optimization_barrier(jnp.mean(gated * gated, -1, keepdims=True)) + eps_norm) * gatenorm_f[None, :]

def finish(outputs, values, c_proj, cumdev, incoming, gate_part, skipgain, gatenorm_f):
    length = values.shape[0]
    values_heads = values.reshape(length, H, P_SIZE)
    from_before = jnp.einsum('tn,hpn->thp', c_proj, incoming, precision=highest) * jnp.exp(cumdev).T[:, :, None]
    ssd_out = outputs + from_before + skipgain[None, :, None] * values_heads
    return gated_norm(ssd_out.reshape(length, H * P_SIZE), gate_part, gatenorm_f)

def mixer(zx_rows, kernels_f, convbias_f, stepbias, decaylog, skipgain, gatenorm_f):
    prior_rows = jnp.zeros((K - 1, CONV), jnp.float32)
    outputs, values, c_proj, cumdev, final_state, decay_total = front(zx_rows[:, DI:], prior_rows, kernels_f, convbias_f, stepbias, decaylog)
    incoming = jnp.zeros((H, P_SIZE, N), jnp.float32)
    return finish(outputs, values, c_proj, cumdev, incoming, zx_rows[:, :DI], skipgain, gatenorm_f)

def adamw_change(weights, gradient, moment_one, moment_two, decay_rate):
    first_new = beta_first * moment_one + (1.0 - beta_first) * gradient
    second_new = beta_second * moment_two + (1.0 - beta_second) * gradient * gradient
    first_hat = first_new / (1.0 - beta_first ** STEP)
    second_hat = second_new / (1.0 - beta_second ** STEP)
    change = -learn_rate * (first_hat / (jnp.sqrt(second_hat) + adam_eps) + decay_rate * weights)
    return (change, first_new, second_new)

def adamw_step(weights, gradient, moment_one, moment_two, decay_rate):
    change, first_new, second_new = adamw_change(weights, gradient, moment_one, moment_two, decay_rate)
    return (weights + change, first_new, second_new)

def reference(hidden_in, out_grad, prenorm, inproj, kernels, convbias, stepbias, decaylog, skipgain, gatenorm, outproj, first_prenorm, second_prenorm, first_inproj, second_inproj, first_kernels, second_kernels, first_convbias, second_convbias, first_stepbias, second_stepbias, first_decaylog, second_decaylog, first_skipgain, second_skipgain, first_gatenorm, second_gatenorm, first_outproj, second_outproj):
    prenorm_b = prenorm.astype(jnp.bfloat16)
    inproj_b = inproj.astype(jnp.bfloat16)
    kernels_b = kernels.astype(jnp.bfloat16)
    convbias_b = convbias.astype(jnp.bfloat16)
    gatenorm_b = gatenorm.astype(jnp.bfloat16)
    outproj_b = outproj.astype(jnp.bfloat16)
    prenorm_f = prenorm_b.astype(jnp.float32)
    kernels_f = kernels_b.astype(jnp.float32)
    convbias_f = convbias_b.astype(jnp.float32)
    gatenorm_f = gatenorm_b.astype(jnp.float32)

    def one_sequence(carried, inputs):
        hidden, cotangent = inputs
        rstd_rows = lax.rsqrt(lax.optimization_barrier(jnp.mean(hidden * hidden, -1, keepdims=True)) + eps_norm)
        normed = hidden * rstd_rows
        normed_b = (normed * prenorm_f[None, :]).astype(jnp.bfloat16)
        zx_rows = jnp.dot(normed_b, inproj_b, preferred_element_type=jnp.float32)
        mixed_f, mixer_back = jax.vjp(mixer, zx_rows, kernels_f, convbias_f, stepbias, decaylog, skipgain, gatenorm_f)
        mixed_b = mixed_f.astype(jnp.bfloat16)
        block_rows = hidden + jnp.dot(mixed_b, outproj_b, preferred_element_type=jnp.float32)
        cot_b = cotangent.astype(jnp.bfloat16)
        g_outproj = jnp.dot(mixed_b.T, cot_b, preferred_element_type=jnp.float32)
        d_mixed = jnp.dot(cot_b, outproj_b.T, preferred_element_type=jnp.float32)
        d_zx, g_kernels, g_convbias, g_stepbias, g_decaylog, g_skipgain, g_gatenorm = mixer_back(d_mixed)
        d_zx_b = d_zx.astype(jnp.bfloat16)
        g_inproj = jnp.dot(normed_b.T, d_zx_b, preferred_element_type=jnp.float32)
        d_normed = jnp.dot(d_zx_b, inproj_b.T, preferred_element_type=jnp.float32)
        g_prenorm = lax.optimization_barrier(jnp.sum(normed * d_normed, axis=0))
        d_hat = d_normed * prenorm_f[None, :]
        hidden_rows = cotangent + rstd_rows * (d_hat - normed * lax.optimization_barrier(jnp.mean(d_hat * normed, -1, keepdims=True)))
        gradients = (g_prenorm, g_inproj, g_kernels, g_convbias, g_stepbias, g_decaylog, g_skipgain, g_gatenorm, g_outproj)
        return (jax.tree.map(jnp.add, carried, gradients), (block_rows, hidden_rows))
    start_sums = (jnp.zeros_like(prenorm), jnp.zeros_like(inproj), jnp.zeros_like(kernels), jnp.zeros_like(convbias), jnp.zeros_like(stepbias), jnp.zeros_like(decaylog), jnp.zeros_like(skipgain), jnp.zeros_like(gatenorm), jnp.zeros_like(outproj))
    totals, (block_out, hidden_grad) = lax.scan(one_sequence, start_sums, (hidden_in, out_grad))
    grad_prenorm, grad_inproj, grad_kernels, grad_convbias, grad_stepbias, grad_decaylog, grad_skipgain, grad_gatenorm, grad_outproj = totals
    change_prenorm, newfirst_prenorm, newsecond_prenorm = adamw_change(prenorm, grad_prenorm, first_prenorm, second_prenorm, 0.0)
    new_inproj, newfirst_inproj, newsecond_inproj = adamw_step(inproj, grad_inproj, first_inproj, second_inproj, decay_matrix)
    change_kernels, newfirst_kernels, newsecond_kernels = adamw_change(kernels, grad_kernels, first_kernels, second_kernels, decay_matrix)
    change_convbias, newfirst_convbias, newsecond_convbias = adamw_change(convbias, grad_convbias, first_convbias, second_convbias, 0.0)
    change_stepbias, newfirst_stepbias, newsecond_stepbias = adamw_change(stepbias, grad_stepbias, first_stepbias, second_stepbias, 0.0)
    change_decaylog, newfirst_decaylog, newsecond_decaylog = adamw_change(decaylog, grad_decaylog, first_decaylog, second_decaylog, 0.0)
    change_skipgain, newfirst_skipgain, newsecond_skipgain = adamw_change(skipgain, grad_skipgain, first_skipgain, second_skipgain, 0.0)
    change_gatenorm, newfirst_gatenorm, newsecond_gatenorm = adamw_change(gatenorm, grad_gatenorm, first_gatenorm, second_gatenorm, 0.0)
    new_outproj, newfirst_outproj, newsecond_outproj = adamw_step(outproj, grad_outproj, first_outproj, second_outproj, decay_matrix)
    return (block_out, hidden_grad, grad_prenorm, grad_inproj, grad_kernels, grad_convbias, grad_stepbias, grad_decaylog, grad_skipgain, grad_gatenorm, grad_outproj, change_prenorm, new_inproj, change_kernels, change_convbias, change_stepbias, change_decaylog, change_skipgain, change_gatenorm, new_outproj, newfirst_prenorm, newsecond_prenorm, newfirst_inproj, newsecond_inproj, newfirst_kernels, newsecond_kernels, newfirst_convbias, newsecond_convbias, newfirst_stepbias, newsecond_stepbias, newfirst_decaylog, newsecond_decaylog, newfirst_skipgain, newsecond_skipgain, newfirst_gatenorm, newsecond_gatenorm, newfirst_outproj, newsecond_outproj)
```

```python
import functools

import jax
import jax.numpy as jnp
from jax import lax
from jax.experimental import pallas as pl
from jax.experimental.pallas import tpu as pltpu
from jax.sharding import PartitionSpec as P

STEP = 4
Q = 128
TILE = 256
LANES = 128

eps_norm = 1e-05
beta_first = 0.9
beta_second = 0.999
adam_eps = 1e-08
learn_rate = 0.01
decay_matrix = 0.1

f32 = jnp.float32
bf16 = jnp.bfloat16
highest = lax.Precision.HIGHEST


def swap_cores(x):
    return lax.ppermute(x, "seq", [(0, 1), (1, 0)])


def swap_dp(x, mask):
    size = lax.axis_size("dp")
    return lax.ppermute(x, "dp", [(i, i ^ mask) for i in range(size)])


def swap_group(x, masks):
    cores, rows, cols = (lax.axis_size(a) for a in ("seq", "dp", "group"))
    pairs = []
    for s in range(cores):
        for d in range(rows):
            for g in range(cols):
                base = (s * rows + d) * cols
                pairs.append((base + g, base + (g ^ masks[s])))
    return lax.ppermute(x, ("seq", "dp", "group"), pairs)


def digits_of(size):
    found, base = [], 1
    while base < size:
        radix = min(4, size // base)
        found.append((base, radix))
        base *= radix
    return found


def per_core(core, pair):
    return jnp.where(core == 0, pair[0], pair[1])


def gather_half(piece):
    core, d, g = (lax.axis_index(a) for a in ("seq", "dp", "group"))
    rows = lax.axis_size("dp")
    cur = piece[None]
    for base, radix in digits_of(rows):
        mine = (d // base) % radix
        got = [cur] + [swap_dp(cur, k * base) for k in range(1, radix)]
        whole = jnp.zeros((radix,) + cur.shape, cur.dtype)
        for k, part in enumerate(got):
            whole = lax.dynamic_update_index_in_dim(whole, part, mine ^ k, 0)
        cur = whole.reshape((radix * cur.shape[0],) + cur.shape[1:])
    first = swap_group(cur, (1, 2))
    both = jnp.stack([cur, first])
    second = swap_group(both, (2, 1))
    whole = jnp.zeros((rows, 4) + piece.shape, piece.dtype)
    places = ((0, 0), (1, 2), (2, 1), (3, 3))
    for part, place in zip((cur, first, second[0], second[1]), places):
        whole = lax.dynamic_update_index_in_dim(whole, part, g ^ per_core(core, place), 1)
    return whole.reshape((rows * 4,) + piece.shape)


def gather_rows(piece):
    core = lax.axis_index("seq")
    half = gather_half(piece)
    other = swap_cores(half)
    whole = jnp.zeros((2,) + half.shape, half.dtype)
    whole = lax.dynamic_update_index_in_dim(whole, half, core, 0)
    whole = lax.dynamic_update_index_in_dim(whole, other, 1 - core, 0)
    return whole.reshape((2 * half.shape[0],) + piece.shape)


def scatter_half(total):
    core, d, g = (lax.axis_index(a) for a in ("seq", "dp", "group"))
    rows = lax.axis_size("dp")
    total = total.reshape((rows, 4) + total.shape[1:])

    def slot(place):
        return lax.dynamic_index_in_dim(total, g ^ per_core(core, place), 1, False)

    send = jnp.stack([slot((1, 2)).astype(bf16), slot((3, 3)).astype(bf16)])
    got = swap_group(send, (1, 2))
    near = slot((0, 0)) + got[0].astype(f32)
    far = slot((2, 1)) + got[1].astype(f32)
    got = swap_group(far.astype(bf16), (2, 1))
    total = near + got.astype(f32)
    for base, radix in reversed(digits_of(rows)):
        total = total.reshape((radix, base) + total.shape[1:])
        mine = (d // base) % radix
        result = lax.dynamic_index_in_dim(total, mine, 0, False)
        for k in range(1, radix):
            part = lax.dynamic_index_in_dim(total, mine ^ k, 0, False).astype(bf16)
            result = result + swap_dp(part, k * base).astype(f32)
        total = result
    return total[0]


def scatter_rows(keep, send):
    return scatter_half(keep + swap_cores(send.astype(bf16)).astype(f32))


def sum_all(x):
    x = x + swap_cores(x)
    for mask in (1, 2):
        x = x + swap_group(x, (mask, mask))
    base = 1
    while base < lax.axis_size("dp"):
        x = x + swap_dp(x, base)
        base *= 2
    return x


def mm(a, b):
    return jnp.dot(a, b, preferred_element_type=f32)


def mm_nt(a, b):
    return lax.dot_general(a, b, (((1,), (1,)), ((), ())), preferred_element_type=f32)


def halves(x):
    hi = x.astype(bf16)
    return hi, (x - hi.astype(f32)).astype(bf16)


def sigmoid(v):
    return 1.0 / (1.0 + jnp.exp(-v))


def softplus(v):
    small = jnp.exp(-jnp.abs(v))
    above = 1.0 + small
    gap = above - 1.0
    log1p = jnp.where(gap == 0.0, small, jnp.log(above) * (small / jnp.where(gap == 0.0, 1.0, gap)))
    return jnp.maximum(v, 0.0) + log1p


def spread(tile, heads_per_tile):
    width = TILE // heads_per_tile
    heads = lax.broadcasted_iota(jnp.int32, (LANES, TILE), 0)
    lanes = lax.broadcasted_iota(jnp.int32, (LANES, TILE), 1)
    return (heads == tile * heads_per_tile + lanes // width).astype(bf16)


def expand(hi, lo, table):
    return mm(hi, table) + mm(lo, table)


def lower(shape=(Q, Q)):
    return lax.broadcasted_iota(jnp.int32, shape, 0) >= lax.broadcasted_iota(jnp.int32, shape, 1)


def front_kernel(
    n_ref, halo_ref, w_ref, ws_ref, taps_ref, cb_ref, sb_ref, dl_ref,
    zin_ref, act_ref, raw_ref, step_ref, cl_ref, hz_ref, fresh_ref, fin_ref,
    zext, bt, tail_hi, tail_lo, ec_hi, ec_lo,
):
    j = pl.program_id(0)
    length = n_ref.shape[0]
    chunks = length // Q
    z = mm(n_ref[...], w_ref[...])
    hz = mm(halo_ref[...], w_ref[...])[8:16]
    zin_ref[...] = z
    hz_ref[...] = hz
    zext[0:8] = hz
    zext[pl.ds(8, length)] = z
    pre = cb_ref[...] + taps_ref[0:1, :] * zext[pl.ds(5, length)]
    for k in range(1, 4):
        pre = pre + taps_ref[k : k + 1, :] * zext[pl.ds(5 + k, length)]
    act = pre * sigmoid(pre)
    act_ref[...] = act

    @pl.when(j == 0)
    def _():
        raw = mm(n_ref[...], ws_ref[...]) + sb_ref[...]
        step = softplus(raw)
        logdec = -step * jnp.exp(dl_ref[...])
        raw_ref[...] = raw
        step_ref[...] = step
        ones = lower().astype(f32)
        ends = []
        for c in range(chunks):
            rows = slice(c * Q, (c + 1) * Q)
            cl = jnp.dot(ones, logdec[rows], precision=highest, preferred_element_type=f32)
            cl_ref[rows] = cl
            end = cl[Q - 1 : Q]
            hi, lo = halves(step[rows] * jnp.exp(end - cl))
            tail_hi[rows] = hi
            tail_lo[rows] = lo
            ends.append(jnp.exp(end))
            bt[c] = act[rows, :LANES].T.astype(bf16)
        ends = jnp.concatenate(ends + [jnp.zeros((8 - chunks, LANES), f32)], axis=0)
        ec_hi[...], ec_lo[...] = halves(ends)

    @pl.when(j > 0)
    def _():
        table = spread(j - 1, 4)
        weights = expand(tail_hi[...], tail_lo[...], table)
        moved_hi, moved_lo = halves(act * weights)
        ends = expand(ec_hi[...], ec_lo[...], table)
        total = None
        for c in range(chunks):
            rows = slice(c * Q, (c + 1) * Q)
            fresh = mm(bt[c], moved_hi[rows]) + mm(bt[c], moved_lo[rows])
            fresh_ref[c] = fresh
            total = fresh if total is None else ends[c : c + 1] * total + fresh
        fin_ref[...] = total.astype(bf16)


def front(n, halo, w, ws, taps, cb, sb, dl, conv):
    length, width = n.shape
    tiles = conv // TILE
    inner = conv - TILE
    chunks = length // Q
    whole = lambda a: pl.BlockSpec(a.shape, lambda j: (0,) * a.ndim)
    col = lambda j: (0, (j + tiles - 1) % tiles)
    late = lambda j: (0, jnp.maximum(j - 1, 0))
    fixed = lambda shape: pl.BlockSpec(shape, lambda j: (0, 0))
    return pl.pallas_call(
        front_kernel,
        grid=(tiles,),
        in_specs=[
            whole(n), whole(halo), pl.BlockSpec((width, TILE), col), whole(ws),
            pl.BlockSpec((4, TILE), col), pl.BlockSpec((1, TILE), col), whole(sb), whole(dl),
        ],
        out_specs=[
            pl.BlockSpec((length, TILE), col), pl.BlockSpec((length, TILE), col),
            fixed((length, LANES)), fixed((length, LANES)), fixed((length, LANES)),
            pl.BlockSpec((8, TILE), col),
            pl.BlockSpec((chunks, LANES, TILE), lambda j: (0,) + late(j)),
            pl.BlockSpec((LANES, TILE), late),
        ],
        out_shape=[
            jax.ShapeDtypeStruct((length, conv), f32),
            jax.ShapeDtypeStruct((length, conv), f32),
            jax.ShapeDtypeStruct((length, LANES), f32),
            jax.ShapeDtypeStruct((length, LANES), f32),
            jax.ShapeDtypeStruct((length, LANES), f32),
            jax.ShapeDtypeStruct((8, conv), f32),
            jax.ShapeDtypeStruct((chunks, LANES, inner), f32),
            jax.ShapeDtypeStruct((LANES, inner), bf16),
        ],
        scratch_shapes=[
            pltpu.VMEM((length + 8, TILE), f32), pltpu.VMEM((chunks, LANES, Q), bf16),
            pltpu.VMEM((length, LANES), bf16), pltpu.VMEM((length, LANES), bf16),
            pltpu.VMEM((8, LANES), bf16), pltpu.VMEM((8, LANES), bf16),
        ],
        cost_estimate=pl.CostEstimate(flops=2 * length * width * conv, bytes_accessed=14 << 20, transcendentals=0),
        name="front",
    )(n, halo, w, ws, taps, cb, sb, dl)


def pair_stack(x):
    first = lax.broadcasted_iota(jnp.int32, x.shape, 1) < LANES // 2
    zero = jnp.zeros_like(x)
    return jnp.concatenate([jnp.where(first, x, zero), jnp.where(first, zero, x)], axis=0)


def scan_kernel(
    v_ref, b_ref, c_ref, step_ref, cl_ref, skip_ref, fresh_ref, inc_ref,
    y_ref, sin_ref,
    gram, clt, cb, st_hi, st_lo, ec_hi, ec_lo, row_hi, row_lo,
):
    j = pl.program_id(0)
    length = v_ref.shape[0]
    chunks = length // Q

    @pl.when(j == 0)
    def _():
        ends = []
        cb[...] = c_ref[...].astype(bf16)
        st_hi[...], st_lo[...] = halves(step_ref[...])
        ec_hi[...], ec_lo[...] = halves(jnp.exp(cl_ref[...]))
        for c in range(chunks):
            rows = slice(c * Q, (c + 1) * Q)
            gram[c] = mm_nt(cb[rows], b_ref[rows].astype(bf16))
            clt[c] = cl_ref[rows].T
            ends.append(jnp.exp(cl_ref[(c + 1) * Q - 1 : (c + 1) * Q]))
        ends = jnp.concatenate(ends + [skip_ref[...], jnp.zeros((7 - chunks, LANES), f32)], axis=0)
        row_hi[...], row_lo[...] = halves(ends)

    table = spread(j, 4)
    steps = expand(st_hi[...], st_lo[...], table)
    grown = expand(ec_hi[...], ec_lo[...], table)
    ends = expand(row_hi[...], row_lo[...], table)
    skip = ends[chunks : chunks + 1]
    cols = pltpu.roll(cl_ref[...], (LANES - 4 * j) % LANES, 1)
    mask = lower()
    state = inc_ref[...].astype(f32)
    for c in range(chunks):
        rows = slice(c * Q, (c + 1) * Q)
        state_b, state_lo = halves(state)
        sin_ref[c] = state_b
        v = v_ref[rows]
        vp = (v * steps[rows]).astype(bf16)
        y = (mm(cb[rows], state_b) + mm(cb[rows], state_lo)) * grown[rows] + skip * v
        parts = []
        for p in range(2):
            mix = []
            for e in range(2):
                i = 2 * p + e
                col = jnp.broadcast_to(cols[rows, i : i + 1], (Q, Q))
                row = clt[c, pl.ds(4 * j + i, 1), :]
                decay = jnp.exp(jnp.where(mask, col - row, -1e30))
                mix.append((decay * gram[c]).astype(bf16))
            parts.append(mm(jnp.concatenate(mix, axis=1), pair_stack(vp[:, p * LANES : (p + 1) * LANES])))
        y_ref[rows] = y + jnp.concatenate(parts, axis=1)
        state = ends[c : c + 1] * state + fresh_ref[c]
    sin_ref[chunks] = state.astype(bf16)


def scan_forward(act, step, cl, skip, fresh, incoming):
    length = act.shape[0]
    inner = incoming.shape[1]
    chunks = length // Q
    tiles = inner // TILE
    whole = lambda a: pl.BlockSpec(a.shape, lambda j: (0,) * a.ndim)
    tile = lambda rows: pl.BlockSpec((rows, TILE), lambda j: (0, j))
    return pl.pallas_call(
        scan_kernel,
        grid=(tiles,),
        in_specs=[
            tile(length),
            pl.BlockSpec((length, LANES), lambda j: (0, inner // LANES)),
            pl.BlockSpec((length, LANES), lambda j: (0, inner // LANES + 1)),
            whole(step), whole(cl), whole(skip),
            pl.BlockSpec((chunks, LANES, TILE), lambda j: (0, 0, j)), tile(LANES),
        ],
        out_specs=[tile(length), pl.BlockSpec((chunks + 1, LANES, TILE), lambda j: (0, 0, j))],
        out_shape=[
            jax.ShapeDtypeStruct((length, inner), f32),
            jax.ShapeDtypeStruct((chunks + 1, LANES, inner), bf16),
        ],
        scratch_shapes=[
            pltpu.VMEM((chunks, Q, Q), f32), pltpu.VMEM((chunks, LANES, Q), f32),
            pltpu.VMEM((length, LANES), bf16),
            pltpu.VMEM((length, LANES), bf16), pltpu.VMEM((length, LANES), bf16),
            pltpu.VMEM((length, LANES), bf16), pltpu.VMEM((length, LANES), bf16),
            pltpu.VMEM((8, LANES), bf16), pltpu.VMEM((8, LANES), bf16),
        ],
        cost_estimate=pl.CostEstimate(flops=4 << 30, bytes_accessed=12 << 20, transcendentals=0),
        name="scan_forward",
    )(act, act, act, step, cl, skip, fresh, incoming)


def state_grad_kernel(dy_ref, c_ref, cl_ref, local_ref, send_ref, ct, ec_hi, ec_lo):
    j = pl.program_id(0)
    length = dy_ref.shape[0]
    chunks = length // Q

    @pl.when(j == 0)
    def _():
        ec_hi[...], ec_lo[...] = halves(jnp.exp(cl_ref[...]))
        for c in range(chunks):
            ct[c] = c_ref[c * Q : (c + 1) * Q].T.astype(bf16)

    grown = expand(ec_hi[...], ec_lo[...], spread(j, 4))
    moved_hi, moved_lo = halves(dy_ref[...].astype(bf16).astype(f32) * grown)
    total = None
    for c in reversed(range(chunks)):
        rows = slice(c * Q, (c + 1) * Q)
        local = mm(ct[c], moved_hi[rows]) + mm(ct[c], moved_lo[rows])
        local_ref[c] = local
        total = local if total is None else local + grown[(c + 1) * Q - 1 : (c + 1) * Q] * total
    send_ref[...] = total.astype(bf16)


def state_grad(dy, act, cl):
    length, inner = dy.shape
    chunks = length // Q
    whole = lambda a: pl.BlockSpec(a.shape, lambda j: (0,) * a.ndim)
    return pl.pallas_call(
        state_grad_kernel,
        grid=(inner // TILE,),
        in_specs=[
            pl.BlockSpec((length, TILE), lambda j: (0, j)),
            pl.BlockSpec((length, LANES), lambda j: (0, inner // LANES + 1)),
            whole(cl),
        ],
        out_specs=[
            pl.BlockSpec((chunks, LANES, TILE), lambda j: (0, 0, j)),
            pl.BlockSpec((LANES, TILE), lambda j: (0, j)),
        ],
        out_shape=[
            jax.ShapeDtypeStruct((chunks, LANES, inner), f32),
            jax.ShapeDtypeStruct((LANES, inner), bf16),
        ],
        scratch_shapes=[
            pltpu.VMEM((chunks, LANES, Q), bf16),
            pltpu.VMEM((length, LANES), bf16), pltpu.VMEM((length, LANES), bf16),
        ],
        cost_estimate=pl.CostEstimate(flops=1 << 29, bytes_accessed=7 << 20, transcendentals=0),
        name="state_grad",
    )(dy, act, cl)


def scan_back_kernel(
    dy_ref, v_ref, y_ref, b_ref, c_ref, step_ref, cl_ref, raw_ref, skip_ref, dl_ref,
    sin_ref, local_ref, dfin_ref,
    dv_ref, db_ref, dc_ref, draw_ref, sums_ref,
    gram, clt, bb, cb, st_hi, st_lo, ec_hi, ec_lo, tl_hi, tl_lo, row_hi, row_lo,
    dgram, q_acc, r_acc, edge, gskip,
):
    j = pl.program_id(0)
    length = dy_ref.shape[0]
    chunks = length // Q

    @pl.when(j == 0)
    def _():
        ends = []
        bb[...] = b_ref[...].astype(bf16)
        cb[...] = c_ref[...].astype(bf16)
        st_hi[...], st_lo[...] = halves(step_ref[...])
        ec_hi[...], ec_lo[...] = halves(jnp.exp(cl_ref[...]))
        for c in range(chunks):
            rows = slice(c * Q, (c + 1) * Q)
            gram[c] = mm_nt(bb[rows], cb[rows])
            cl = cl_ref[rows]
            clt[c] = cl.T
            end = cl[Q - 1 : Q]
            tl_hi[rows], tl_lo[rows] = halves(jnp.exp(end - cl))
            ends.append(jnp.exp(end))
        ends = jnp.concatenate(ends + [skip_ref[...], jnp.zeros((7 - chunks, LANES), f32)], axis=0)
        row_hi[...], row_lo[...] = halves(ends)
        dgram[...] = jnp.zeros_like(dgram)
        q_acc[...] = jnp.zeros_like(q_acc)
        r_acc[...] = jnp.zeros_like(r_acc)
        edge[...] = jnp.zeros_like(edge)
        gskip[...] = jnp.zeros_like(gskip)
        db_ref[...] = jnp.zeros_like(db_ref)
        dc_ref[...] = jnp.zeros_like(dc_ref)

    table = spread(j, 4)
    steps = expand(st_hi[...], st_lo[...], table)
    grown = expand(ec_hi[...], ec_lo[...], table)
    tails = expand(tl_hi[...], tl_lo[...], table)
    ends = expand(row_hi[...], row_lo[...], table)
    skip = ends[chunks : chunks + 1]
    cols = pltpu.roll(cl_ref[...], (LANES - 4 * j) % LANES, 1)
    upper = lax.broadcasted_iota(jnp.int32, (Q, Q), 0) <= lax.broadcasted_iota(jnp.int32, (Q, Q), 1)

    def heads(x):
        hi, lo = halves(x)
        return mm_nt(hi, table) + mm_nt(lo, table)

    dstate = dfin_ref[...].astype(f32)
    edge[...] += heads(jnp.sum((dstate * sin_ref[chunks].astype(f32)).reshape(16, 8, TILE), axis=0))
    skips = jnp.zeros((8, TILE), f32)
    for c in reversed(range(chunks)):
        rows = slice(c * Q, (c + 1) * Q)
        dy = dy_ref[rows]
        v = v_ref[rows]
        dy_b = dy.astype(bf16)
        vp = v * steps[rows]
        vp_b = vp.astype(bf16)
        dstate_b, dstate_lo = halves(dstate)
        parts = []
        dg = dgram[c]
        for p in range(2):
            lanes = slice(p * LANES, (p + 1) * LANES)
            dmix = mm_nt(pair_stack(vp_b[:, lanes]), dy_b[:, lanes])
            mix = []
            for e in range(2):
                i = 2 * p + e
                col = jnp.broadcast_to(cols[rows, i : i + 1], (Q, Q))
                row = clt[c, pl.ds(4 * j + i, 1), :]
                decay = jnp.exp(jnp.where(upper, row - col, -1e30))
                mix.append((decay * gram[c]).astype(bf16))
                dg = dg + decay * dmix[e * Q : (e + 1) * Q]
            parts.append(mm(jnp.concatenate(mix, axis=1), pair_stack(dy_b[:, lanes])))
        dgram[c] = dg
        tail = tails[rows]
        inside = jnp.concatenate(parts, axis=1)
        across = (mm(bb[rows], dstate_b) + mm(bb[rows], dstate_lo)) * tail
        dvp = inside + across
        db_ref[rows] += mm_nt((vp * tail).astype(bf16), dstate_b)
        dc_ref[rows] += mm_nt((dy * grown[rows]).astype(bf16), sin_ref[c])
        dv_ref[rows] = steps[rows] * dvp + skip * dy
        q_acc[rows] += heads(
            dy_b.astype(f32) * (y_ref[rows] - skip * v) - inside * vp_b.astype(f32) - across * vp
        )
        r_acc[rows] += heads(dvp * v)
        skips = skips + jnp.sum((dy * v).reshape(Q // 8, 8, TILE), axis=0)
        dstate = local_ref[c] + ends[c : c + 1] * dstate
    gskip[...] += heads(skips)

    @pl.when(j == pl.num_programs(0) - 1)
    def _():
        ones = lower().astype(f32)
        dec = jnp.exp(dl_ref[...])
        after = jnp.sum(edge[...], axis=0, keepdims=True)
        g_dl = jnp.zeros((1, LANES), f32)
        g_sb = jnp.zeros((1, LANES), f32)
        for c in reversed(range(chunks)):
            rows = slice(c * Q, (c + 1) * Q)
            dg = dgram[c]
            db_ref[rows] += mm(dg.astype(bf16), cb[rows])
            dc_ref[rows] += mm(dg.T.astype(bf16), bb[rows])
            q = q_acc[rows]
            dlog = after + lax.dot_general(
                ones, q, (((0,), (0,)), ((), ())), precision=highest, preferred_element_type=f32
            )
            after = after + jnp.sum(q, axis=0, keepdims=True)
            step = step_ref[rows]
            g_dl = g_dl + jnp.sum(dlog * (-step * dec), axis=0, keepdims=True)
            draw = (r_acc[rows] - dlog * dec) * sigmoid(raw_ref[rows])
            draw_ref[rows] = draw
            g_sb = g_sb + jnp.sum(draw, axis=0, keepdims=True)
        g_skip = jnp.sum(gskip[...], axis=0, keepdims=True)
        sums_ref[...] = jnp.concatenate([g_sb, g_dl, g_skip, jnp.zeros((5, LANES), f32)], axis=0)


def scan_backward(dy, act, y, step, cl, raw, skip, dl, states, local, dfin):
    length, inner = dy.shape
    chunks = length // Q
    whole = lambda a: pl.BlockSpec(a.shape, lambda j: (0,) * a.ndim)
    tile = lambda rows: pl.BlockSpec((rows, TILE), lambda j: (0, j))
    fixed = lambda shape: pl.BlockSpec(shape, lambda j: (0, 0))
    row = pltpu.VMEM((length, LANES), bf16)
    return pl.pallas_call(
        scan_back_kernel,
        grid=(inner // TILE,),
        in_specs=[
            tile(length), tile(length), tile(length),
            pl.BlockSpec((length, LANES), lambda j: (0, inner // LANES)),
            pl.BlockSpec((length, LANES), lambda j: (0, inner // LANES + 1)),
            whole(step), whole(cl), whole(raw), whole(skip), whole(dl),
            pl.BlockSpec((chunks + 1, LANES, TILE), lambda j: (0, 0, j)),
            pl.BlockSpec((chunks, LANES, TILE), lambda j: (0, 0, j)),
            tile(LANES),
        ],
        out_specs=[tile(length), fixed((length, LANES)), fixed((length, LANES)), fixed((length, LANES)), fixed((8, LANES))],
        out_shape=[
            jax.ShapeDtypeStruct((length, inner), f32),
            jax.ShapeDtypeStruct((length, LANES), f32),
            jax.ShapeDtypeStruct((length, LANES), f32),
            jax.ShapeDtypeStruct((length, LANES), f32),
            jax.ShapeDtypeStruct((8, LANES), f32),
        ],
        scratch_shapes=[
            pltpu.VMEM((chunks, Q, Q), f32), pltpu.VMEM((chunks, LANES, Q), f32),
            row, row, row, row, row, row, row, row,
            pltpu.VMEM((8, LANES), bf16), pltpu.VMEM((8, LANES), bf16),
            pltpu.VMEM((chunks, Q, Q), f32),
            pltpu.VMEM((length, LANES), f32), pltpu.VMEM((length, LANES), f32),
            pltpu.VMEM((8, LANES), f32), pltpu.VMEM((8, LANES), f32),
        ],
        cost_estimate=pl.CostEstimate(flops=8 << 30, bytes_accessed=20 << 20, transcendentals=0),
        name="scan_backward",
    )(dy, act, y, act, act, step, cl, raw, skip, dl, states, local, dfin)


def conv_back_kernel(
    dv_ref, db_ref, dc_ref, zin_ref, hz_ref, taps_ref, cb_ref,
    dz_ref, last_ref, head_ref, gw_ref, gb_ref,
    zext, dext,
):
    j = pl.program_id(0)
    length = zin_ref.shape[0]
    zext[0:8] = hz_ref[...]
    zext[pl.ds(8, length)] = zin_ref[...]
    pre = cb_ref[...] + taps_ref[0:1, :] * zext[pl.ds(5, length)]
    for k in range(1, 4):
        pre = pre + taps_ref[k : k + 1, :] * zext[pl.ds(5 + k, length)]
    sig = sigmoid(pre)
    slope = sig * (1.0 + pre * (1.0 - sig))
    last = pl.num_programs(0) - 1

    @pl.when(j < last)
    def _():
        dext[pl.ds(0, length)] = dv_ref[...] * slope

    @pl.when(j == last)
    def _():
        dext[pl.ds(0, length), :LANES] = db_ref[...] * slope[:, :LANES]
        dext[pl.ds(0, length), LANES:] = dc_ref[...] * slope[:, LANES:]

    dext[pl.ds(length, 8)] = jnp.zeros((8, TILE), f32)
    dpre = dext[pl.ds(0, length)]
    head_ref[...] = dpre[0:8]
    gb_ref[...] = jnp.sum(dpre, axis=0, keepdims=True)
    dz = taps_ref[3:4, :] * dpre
    sums = []
    for k in range(4):
        sums.append(jnp.sum(dpre * zext[pl.ds(5 + k, length)], axis=0, keepdims=True))
        if k < 3:
            dz = dz + taps_ref[k : k + 1, :] * dext[pl.ds(3 - k, length)]
    gw_ref[...] = jnp.concatenate(sums, axis=0)
    dz_ref[...] = dz.astype(bf16)
    last_ref[...] = dz[length - 16 :]


def conv_backward(dv, db, dc, zin, hz, taps, cb):
    length, conv = zin.shape
    tiles = conv // TILE
    col = lambda rows: pl.BlockSpec((rows, TILE), lambda j: (0, j))
    whole = lambda a: pl.BlockSpec(a.shape, lambda j: (0,) * a.ndim)
    return pl.pallas_call(
        conv_back_kernel,
        grid=(tiles,),
        in_specs=[
            pl.BlockSpec((length, TILE), lambda j: (0, jnp.minimum(j, tiles - 2))),
            whole(db), whole(dc), col(length), col(8), col(4), col(1),
        ],
        out_specs=[col(length), col(16), col(8), col(4), col(1)],
        out_shape=[
            jax.ShapeDtypeStruct((length, conv), bf16),
            jax.ShapeDtypeStruct((16, conv), f32),
            jax.ShapeDtypeStruct((8, conv), f32),
            jax.ShapeDtypeStruct((4, conv), f32),
            jax.ShapeDtypeStruct((1, conv), f32),
        ],
        scratch_shapes=[pltpu.VMEM((length + 8, TILE), f32), pltpu.VMEM((length + 8, TILE), f32)],
        cost_estimate=pl.CostEstimate(flops=1 << 29, bytes_accessed=12 << 20, transcendentals=0),
        name="conv_backward",
    )(dv, db, dc, zin, hz, taps, cb)


def adamw_change(weights, gradient, moment_one, moment_two, decay_rate):
    first_new = beta_first * moment_one + (1.0 - beta_first) * gradient
    second_new = beta_second * moment_two + (1.0 - beta_second) * gradient * gradient
    first_hat = first_new / (1.0 - beta_first**STEP)
    second_hat = second_new / (1.0 - beta_second**STEP)
    change = -learn_rate * (first_hat / (jnp.sqrt(second_hat) + adam_eps) + decay_rate * weights)
    return (change, first_new, second_new)


def adamw_step(weights, gradient, moment_one, moment_two, decay_rate):
    change, first_new, second_new = adamw_change(
        weights, gradient, moment_one, moment_two, decay_rate
    )
    return (weights + change, first_new, second_new)


def tn(a, b):
    return lax.dot_general(a, b, (((0,), (0,)), ((), ())), preferred_element_type=f32)


def nt(a, b):
    return lax.dot_general(a, b, (((1,), (1,)), ((), ())), preferred_element_type=f32)


def pad_heads(x):
    return jnp.pad(x, (0, LANES - x.shape[0]))[None]


def on_device(
    hidden_in, out_grad, prenorm, inproj, kernels, convbias, stepbias, decaylog, skipgain,
    gatenorm, outproj, first_prenorm, second_prenorm, first_inproj, second_inproj,
    first_kernels, second_kernels, first_convbias, second_convbias, first_stepbias,
    second_stepbias, first_decaylog, second_decaylog, first_skipgain, second_skipgain,
    first_gatenorm, second_gatenorm, first_outproj, second_outproj,
):
    core = lax.axis_index("seq")
    devices = lax.axis_size("seq") * lax.axis_size("dp") * lax.axis_size("group")
    half = devices // 2
    heads = stepbias.shape[0]
    taps_n, ch = kernels.shape
    conv = ch * devices
    gn = gatenorm.shape[0]
    pn = prenorm.shape[0]
    inner = gn * devices
    width = pn * devices
    tokens = hidden_in[0]
    cotangent = out_grad[0]

    small = jnp.concatenate([prenorm, kernels.reshape(-1), convbias, gatenorm]).astype(bf16)
    used = small.shape[0]
    rows = -(-used // (8 * LANES)) * 8
    small = jnp.pad(small, (0, rows * LANES - used)).reshape(rows, LANES)
    small = gather_rows(small).reshape(devices, rows * LANES)
    cut = [0, pn, pn + taps_n * ch, pn + (taps_n + 1) * ch, used]
    prenorm_f = small[:, : cut[1]].reshape(width).astype(f32)
    kernels_f = small[:, cut[1] : cut[2]].reshape(devices, taps_n, ch).transpose(1, 0, 2)
    kernels_f = kernels_f.reshape(taps_n, conv).astype(f32)
    convbias_f = small[:, cut[2] : cut[3]].reshape(1, conv).astype(f32)
    gatenorm_f = small[:, cut[3] : cut[4]].reshape(1, inner).astype(f32)

    inproj_b = inproj.astype(bf16)
    w_conv = gather_rows(inproj_b[:, inner:]).reshape(width, conv + heads)
    w_gate = gather_rows(inproj_b[:, :inner]).reshape(width, inner)
    w_out = gather_rows(outproj.astype(bf16)).reshape(inner, width)

    before = lax.ppermute(tokens[-16:], "seq", [(0, 1)])

    def norm(x):
        rstd = lax.rsqrt(jnp.mean(x * x, -1, keepdims=True) + eps_norm)
        return x * rstd, rstd

    normed, rstd = norm(tokens)
    normed_b = (normed * prenorm_f[None]).astype(bf16)
    halo_b = (norm(before)[0] * prenorm_f[None]).astype(bf16)

    sb, dl, skip = pad_heads(stepbias), pad_heads(decaylog), pad_heads(skipgain)
    w_step = jnp.pad(w_conv[:, conv:], ((0, 0), (0, LANES - heads)))
    zin, act, raw, step, cl, hz, fresh, final = front(
        normed_b, halo_b, w_conv, w_step, kernels_f, convbias_f, sb, dl, conv
    )
    incoming = lax.ppermute(final, "seq", [(0, 1)])
    y, states = scan_forward(act, step, cl, skip, fresh, incoming)

    gate = jnp.dot(normed_b, w_gate, preferred_element_type=f32)
    sig = sigmoid(gate)
    gated = y * (gate * sig)
    rms = lax.rsqrt(jnp.mean(gated * gated, -1, keepdims=True) + eps_norm)
    unit = gated * rms
    mixed_b = (unit * gatenorm_f).astype(bf16)
    block_rows = tokens + jnp.dot(mixed_b, w_out, preferred_element_type=f32)
    cot_b = cotangent.astype(bf16)
    d_mixed = nt(cot_b, w_out)

    def own(a, mine):
        start = jnp.where(mine, core, 1 - core) * (a.shape[1] // 2)
        return lax.dynamic_slice_in_dim(a, start, a.shape[1] // 2, 1)

    send = tn(own(mixed_b, False), cot_b).reshape(half, gn, width)
    keep = tn(own(mixed_b, True), cot_b).reshape(half, gn, width)
    grad_outproj = scatter_rows(keep, send)

    d_unit = d_mixed * gatenorm_f
    d_gated = rms * (d_unit - unit * jnp.mean(d_unit * unit, -1, keepdims=True))
    d_y = d_gated * (gate * sig)
    d_gate_b = (d_gated * y * (sig * (1.0 + gate * (1.0 - sig)))).astype(bf16)

    local, d_in = state_grad(d_y, act, cl)
    d_final = lax.ppermute(d_in, "seq", [(1, 0)])
    send = tn(own(normed_b, False), d_gate_b).reshape(half, pn, inner)
    keep = tn(own(normed_b, True), d_gate_b).reshape(half, pn, inner)
    grad_gatecols = scatter_rows(keep, send)

    dv, db, dc, draw, sums = scan_backward(d_y, act, y, step, cl, raw, skip, dl, states, local, d_final)
    dz, last, head, g_kernels, g_convbias = conv_backward(dv, db, dc, zin, hz, kernels_f, convbias_f)
    nxt = lax.ppermute(head, "seq", [(1, 0)])
    reach = taps_n - 1
    fix = []
    for i in range(reach):
        fix.append(sum(kernels_f[k] * nxt[i - k] for k in range(i + 1)))
    last = last.at[-reach:].add(jnp.stack(fix))
    dz = lax.dynamic_update_slice(dz, last.astype(bf16), (dz.shape[0] - 16, 0))
    dz = jnp.concatenate([dz, draw[:, :heads].astype(bf16)], axis=1)

    extra = jnp.concatenate(
        [
            g_kernels.reshape(taps_n, devices, ch).transpose(1, 0, 2).reshape(devices, taps_n * ch),
            g_convbias.reshape(devices, ch),
        ],
        axis=1,
    )
    wide = -(-extra.shape[1] // pn)
    extra = jnp.pad(extra, ((0, 0), (0, wide * pn - extra.shape[1]))).reshape(2, half, pn, wide)
    send = tn(own(normed_b, False), dz).reshape(half, pn, conv + heads)
    keep = tn(own(normed_b, True), dz).reshape(half, pn, conv + heads)
    pick = lambda s: lax.dynamic_index_in_dim(extra, s, 0, False)
    send = jnp.concatenate([send, pick(1 - core)], axis=2)
    keep = jnp.concatenate([keep, pick(core)], axis=2)
    grad_last = scatter_rows(keep, send)

    d_normed = nt(d_gate_b, w_gate) + nt(dz, w_conv)
    d_hat = d_normed * prenorm_f[None]
    hidden_rows = cotangent + rstd * (
        d_hat - normed * jnp.mean(d_hat * normed, -1, keepdims=True)
    )

    grad_inproj = jnp.concatenate([grad_gatecols, grad_last[:, : conv + heads]], axis=1)
    flat = grad_last[:, conv + heads :].reshape(-1)
    grad_kernels = flat[: taps_n * ch].reshape(taps_n, ch)
    grad_convbias = flat[taps_n * ch : (taps_n + 1) * ch]
    grad_prenorm = jnp.sum(grad_inproj * inproj_b.astype(f32), axis=1) / prenorm.astype(bf16).astype(f32)
    grad_gatenorm = jnp.sum(
        grad_outproj * outproj.astype(bf16).astype(f32), axis=1
    ) / gatenorm.astype(bf16).astype(f32)
    totals = sum_all(sums)
    grad_stepbias, grad_decaylog, grad_skipgain = (totals[i, :heads] for i in range(3))

    change_prenorm, newfirst_prenorm, newsecond_prenorm = adamw_change(
        prenorm, grad_prenorm, first_prenorm, second_prenorm, 0.0
    )
    new_inproj, newfirst_inproj, newsecond_inproj = adamw_step(
        inproj, grad_inproj, first_inproj, second_inproj, decay_matrix
    )
    change_kernels, newfirst_kernels, newsecond_kernels = adamw_change(
        kernels, grad_kernels, first_kernels, second_kernels, decay_matrix
    )
    change_convbias, newfirst_convbias, newsecond_convbias = adamw_change(
        convbias, grad_convbias, first_convbias, second_convbias, 0.0
    )
    change_stepbias, newfirst_stepbias, newsecond_stepbias = adamw_change(
        stepbias, grad_stepbias, first_stepbias, second_stepbias, 0.0
    )
    change_decaylog, newfirst_decaylog, newsecond_decaylog = adamw_change(
        decaylog, grad_decaylog, first_decaylog, second_decaylog, 0.0
    )
    change_skipgain, newfirst_skipgain, newsecond_skipgain = adamw_change(
        skipgain, grad_skipgain, first_skipgain, second_skipgain, 0.0
    )
    change_gatenorm, newfirst_gatenorm, newsecond_gatenorm = adamw_change(
        gatenorm, grad_gatenorm, first_gatenorm, second_gatenorm, 0.0
    )
    new_outproj, newfirst_outproj, newsecond_outproj = adamw_step(
        outproj, grad_outproj, first_outproj, second_outproj, decay_matrix
    )
    return (
        block_rows[None], hidden_rows[None],
        grad_prenorm, grad_inproj, grad_kernels, grad_convbias, grad_stepbias, grad_decaylog,
        grad_skipgain, grad_gatenorm, grad_outproj,
        change_prenorm, new_inproj, change_kernels, change_convbias, change_stepbias,
        change_decaylog, change_skipgain, change_gatenorm, new_outproj,
        newfirst_prenorm, newsecond_prenorm, newfirst_inproj, newsecond_inproj,
        newfirst_kernels, newsecond_kernels, newfirst_convbias, newsecond_convbias,
        newfirst_stepbias, newsecond_stepbias, newfirst_decaylog, newsecond_decaylog,
        newfirst_skipgain, newsecond_skipgain, newfirst_gatenorm, newsecond_gatenorm,
        newfirst_outproj, newsecond_outproj,
    )


def solution(mesh):
    tokens = P(("dp", "group"), "seq", None)
    vec = P(("seq", "dp", "group"))
    mat = P(("seq", "dp", "group"), None)
    cols = P(None, ("seq", "dp", "group"))
    rep = P()
    each = (vec, mat, cols, vec, rep, rep, rep, vec, mat)
    moments = tuple(s for s in each for _ in range(2))
    return jax.shard_map(
        on_device,
        mesh=mesh,
        in_specs=(tokens, tokens) + each + moments,
        out_specs=(tokens, tokens) + each + each + moments,
        check_vma=False,
    )
```
